256 devices in a mesh: grp: 16 (over y_hi, x, core), pose: 16 (over y_lo, z).
Axes of the slice: x: 4, y: 4 (y_hi: 2, y_lo: 2; y = y_hi * 2 + y_lo), z: 8, core: 2. Of those that a mesh axis runs over, the one named last changes fastest.
Arguments:
- particles: bfloat16 [81920, 16384], P(('grp', 'pose')), may hold values from -64 to 64
- projections: bfloat16 [128, 16384], P('pose'), may hold values from -1.5 to 1.5
- ctf_table: bfloat16 [32, 16384], replicated, may hold values from 0.099609375 to 1
- group_ids: int32 [81920], P(('grp', 'pose')), may hold values from 0 to 31
Outputs:
- gradient: float32 [128, 16384], P('pose', 'grp')
- log_norm: float32 [81920], P(('grp', 'pose'))
The draws below stay inside these ranges and needn't reach their ends.
All inputs are finite; a program needn't handle non-finite values.
Results may differ from the reference program's by a relative error of at most 0.0065.
Values may be sent and summed in bfloat16 or wider, within the bound.
No kernel may reach another device: no remote copies, remote signals or barrier semaphores. Data moves between devices by JAX's collectives and lax.ppermute only.
A program may use at most 128 MiB of HBM per device.

```python
import math
import jax
import jax.numpy as jnp
from jax import lax

F = 16384
PART_DEV = 320
GROUPS = 32
POSES = 128
PARTICLES = 81920


def projection_values(key):
    return 0.25 * jax.random.truncated_normal(jax.random.fold_in(key, 11), -6.0, 6.0, (POSES, F), jnp.float32)


def draw_projections(key, part):
    return projection_values(key).astype(jnp.bfloat16)


def draw_particles(key, part):
    own_key = jax.random.fold_in(key, 23)
    key_noise = jax.random.fold_in(own_key, 0)
    key_first = jax.random.fold_in(own_key, 2)
    model_rows = projection_values(key)
    first_pose = jax.random.randint(key_first, (PARTICLES,), 0, POSES)
    signal = model_rows[first_pose]
    noise_term = jax.random.truncated_normal(key_noise, -6.0, 6.0, (PARTICLES, F), jnp.float32)
    values = 0.5 * signal + noise_term
    return values.astype(jnp.bfloat16)


def plant(result, key, low, largest):
    longest = result.shape.index(max(result.shape))
    spots = []
    for shift in (0, 1):
        where = [jax.random.randint(jax.random.fold_in(key, axis), (), 0, length) for axis, length in enumerate(result.shape)]
        where[longest] = (where[longest] + shift) % result.shape[longest]
        spots.append(tuple(where))
    return result.at[spots[0]].set(low).at[spots[1]].set(largest)


def setup_inputs(seed: int = 0) -> dict:
    seeds = jax.random.split(jax.random.key(seed), 5)
    particles = draw_particles(jax.random.fold_in(seeds[4], 71), 0)
    projections = draw_projections(jax.random.fold_in(seeds[4], 71), 0)
    ctf_table = jnp.clip(jax.random.uniform(seeds[2], (GROUPS, F), jnp.float32, 0.099609375, 1.0), 0.099609375, 1.0).astype(jnp.bfloat16)
    group_ids = plant(jax.random.randint(seeds[3], (PARTICLES,), 0, GROUPS), jax.random.fold_in(seeds[3], 1), 0, GROUPS - 1).astype(jnp.int32)
    return dict(particles=particles, projections=projections, ctf_table=ctf_table, group_ids=group_ids)


def reference(particles, projections, ctf_table, group_ids):
    high = lax.Precision.HIGHEST
    inverse = 4.0 / math.sqrt(F)
    model_f32 = projections.astype(jnp.float32)
    ctf_square = jnp.square(ctf_table.astype(jnp.float32))
    norms = jnp.dot(ctf_square, (model_f32 * model_f32).T, precision=high)
    block_count = PARTICLES // PART_DEV
    part_blocks = particles.reshape(block_count, PART_DEV, F)
    id_blocks = group_ids.reshape(block_count, PART_DEV)

    def block_step(carried, slice_item):
        numerator, pose_mass = carried
        part_rows, part_ids = slice_item
        ctf_rows = ctf_table[part_ids].astype(jnp.float32)
        weighted = lax.optimization_barrier((ctf_rows * part_rows.astype(jnp.float32)).astype(jnp.bfloat16))
        weighted_f32 = weighted.astype(jnp.float32)
        raw_dots = jnp.dot(weighted_f32, model_f32.T, precision=high)
        one_hot = (part_ids[:, None] == jnp.arange(GROUPS, dtype=jnp.int32)[None, :]).astype(jnp.float32)
        picked = jnp.dot(one_hot, norms, precision=high)
        scores = inverse * (raw_dots - 0.5 * picked)
        row_peak = lax.optimization_barrier(jnp.max(scores, axis=1, keepdims=True))
        log_norm = row_peak[:, 0] + jnp.log(lax.optimization_barrier(jnp.sum(jnp.exp(scores - row_peak), axis=1)))
        weights = lax.optimization_barrier(jnp.exp(scores - log_norm[:, None]).astype(jnp.bfloat16))
        weights_f32 = weights.astype(jnp.float32)
        numerator = numerator + jnp.dot(weights_f32.T, weighted_f32, precision=high)
        pose_mass = pose_mass + jnp.dot(weights_f32.T, one_hot, precision=high)
        return ((numerator, pose_mass), log_norm)
    start_state = (jnp.zeros((POSES, F), jnp.float32), jnp.zeros((POSES, GROUPS), jnp.float32))
    (numerator, pose_mass), log_blocks = lax.scan(block_step, start_state, (part_blocks, id_blocks))
    factor = POSES / PARTICLES
    gradient = factor * (numerator - model_f32 * jnp.dot(pose_mass, ctf_square, precision=high))
    return (gradient, log_blocks.reshape(PARTICLES))
```

```python
import functools
import math

import jax
import jax.numpy as jnp
from jax import lax
from jax.experimental import pallas as pl
from jax.experimental.pallas import tpu as pltpu
from jax.sharding import PartitionSpec as P

NAMES = ("yh", "x", "core", "yl", "z")
BLK = 1024
BF = jnp.bfloat16
F32 = jnp.float32


def dot_tn(a, b):
    return lax.dot_general(a, b, (((0,), (0,)), ((), ())), preferred_element_type=F32)


def dot_nt(a, b):
    return lax.dot_general(a, b, (((1,), (1,)), ((), ())), preferred_element_type=F32)


def one_hot_t(ids, groups):
    rows = lax.broadcasted_iota(jnp.int32, (groups, ids.shape[1]), 0)
    return jnp.where(rows == ids, 1.0, 0.0).astype(BF)


def split2(v):
    hi = v.astype(BF)
    return hi, (v - hi.astype(F32)).astype(BF)


def split3(v):
    hi = v.astype(BF)
    rest = v - hi.astype(F32)
    mid = rest.astype(BF)
    return hi, mid, (rest - mid.astype(F32)).astype(BF)


def weighted_kernel(par_ref, ids_ref, ctf_ref, part_ref, out_ref):
    hot = one_hot_t(ids_ref[...], ctf_ref.shape[0])
    rows = dot_tn(hot, ctf_ref[...])
    out_ref[...] = (rows * part_ref[...].astype(F32)).astype(BF)


def weighted_call(parity, ids, ctf, particles):
    n, f = particles.shape
    g = ctf.shape[0]
    nb = f // BLK // 2
    return pl.pallas_call(
        weighted_kernel,
        grid_spec=pltpu.PrefetchScalarGridSpec(
            num_scalar_prefetch=1,
            grid=(nb,),
            in_specs=[
                pl.BlockSpec((1, n), lambda j, p: (0, 0)),
                pl.BlockSpec((g, BLK), lambda j, p: (0, 2 * j + p[0])),
                pl.BlockSpec((n, BLK), lambda j, p: (0, 2 * j + p[0])),
            ],
            out_specs=pl.BlockSpec((n, BLK), lambda j, p: (0, j)),
        ),
        out_shape=jax.ShapeDtypeStruct((n, f // 2), BF),
    )(parity, ids, ctf, particles)


def score_kernel(par_ref, wa_ref, wb_ref, proj_ref, ctf_ref, s_ref, n_ref):
    j = pl.program_id(0)
    n = wa_ref.shape[0]
    g = ctf_ref.shape[0]
    proj = proj_ref[...]
    poses = proj.shape[0]
    da = dot_nt(wa_ref[...], proj)
    db = dot_nt(wb_ref[...], proj)
    c = ctf_ref[...].astype(F32)
    pf = proj.astype(F32)
    ch, cl = split2(c * c)
    ph, plo = split2(pf * pf)
    quad = dot_nt(jnp.concatenate([ch, cl], axis=0), jnp.concatenate([ph, plo], axis=0))
    dn = (quad[:g, :poses] + quad[g:, :poses]) + (quad[:g, poses:] + quad[g:, poses:])

    @pl.when(j == 0)
    def _():
        s_ref[:n, :] = da
        s_ref[n:, :] = db
        n_ref[...] = dn

    @pl.when(j > 0)
    def _():
        s_ref[:n, :] += da
        s_ref[n:, :] += db
        n_ref[...] += dn


def score_call(parity, wa, wb, proj, ctf):
    n, f = wa.shape
    g = ctf.shape[0]
    poses = proj.shape[0]
    return pl.pallas_call(
        score_kernel,
        grid_spec=pltpu.PrefetchScalarGridSpec(
            num_scalar_prefetch=1,
            grid=(f // BLK,),
            in_specs=[
                pl.BlockSpec((n, BLK), lambda j, p: (0, j)),
                pl.BlockSpec((n, BLK), lambda j, p: (0, j)),
                pl.BlockSpec((poses, BLK), lambda j, p: (0, j)),
                pl.BlockSpec((g, BLK), lambda j, p: (0, 2 * j + p[0])),
            ],
            out_specs=[
                pl.BlockSpec((2 * n, poses), lambda j, p: (0, 0)),
                pl.BlockSpec((g, poses), lambda j, p: (0, 0)),
            ],
        ),
        out_shape=[
            jax.ShapeDtypeStruct((2 * n, poses), F32),
            jax.ShapeDtypeStruct((g, poses), F32),
        ],
    )(parity, wa, wb, proj, ctf)


def softmax_kernel(inverse, ids_ref, *refs):
    s0, r0, s1, r1, n0, m0, n1, m1, log_ref, w_ref, mass_ref = refs
    g = n0.shape[0]
    raw = jnp.concatenate([s0[...] + r0[...], s1[...] + r1[...]], axis=1)
    norms = jnp.concatenate([n0[...] + m0[...], n1[...] + m1[...]], axis=1)
    hot = one_hot_t(ids_ref[...], g)
    picked = dot_tn(jnp.concatenate([hot, hot, hot], axis=0), jnp.concatenate(split3(norms), axis=0))
    scores = inverse * (raw - 0.5 * picked)
    peak = jnp.max(scores, axis=1, keepdims=True)
    log_norm = peak + jnp.log(jnp.sum(jnp.exp(scores - peak), axis=1, keepdims=True))
    weights = jnp.exp(scores - log_norm).astype(BF)
    log_ref[...] = log_norm[: log_ref.shape[0], :]
    w_ref[...] = weights
    mass_ref[...] = jnp.dot(hot, weights, preferred_element_type=F32)


def softmax_call(inverse, ids, parts):
    rows = ids.shape[1]
    poses = 2 * parts[0].shape[1]
    g = parts[4].shape[0]
    return pl.pallas_call(
        functools.partial(softmax_kernel, inverse),
        out_shape=[
            jax.ShapeDtypeStruct((rows // 2, 1), F32),
            jax.ShapeDtypeStruct((rows, poses), BF),
            jax.ShapeDtypeStruct((g, poses), F32),
        ],
    )(ids, *parts)


def gradient_kernel(by_y, jt_ref, w_ref, mass_ref, wa_ref, wb_ref, p0_ref, p1_ref, ctf_ref, *outs):
    s = pl.program_id(0)
    a, dx = s // 4, s % 4
    n = wa_ref.shape[0]
    acc = dot_tn(w_ref[:n, :], wa_ref[...]) + dot_tn(w_ref[n:, :], wb_ref[...])
    c = ctf_ref[...].astype(F32)
    ch, cl = split2(c * c)
    mh, mm, ml = split3(mass_ref[...])
    corr = dot_tn(
        jnp.concatenate([mh, mh, mm, mm, ml], axis=0), jnp.concatenate([ch, cl, ch, cl, ch], axis=0)
    )
    half = p0_ref.shape[0]
    top = acc[:half] - p0_ref[...].astype(F32) * corr[:half]
    low = acc[half:] - p1_ref[...].astype(F32) * corr[half:]
    if by_y:
        for at in range(2):

            @pl.when(a == at)
            def _(at=at):
                for b, v in ((0, top), (1, low)):
                    ref = outs[2 * at + b]
                    ref[dx] = v.astype(ref.dtype)
    else:
        for at in range(4):

            @pl.when(dx == at)
            def _(at=at):
                ref = outs[at]
                ref[a, 0] = top.astype(ref.dtype)
                ref[a, 1] = low.astype(ref.dtype)


def gradient_call(by_y, jt, weights, mass, wa, wb, p0, p1, ctf):
    n, f = wa.shape
    g = ctf.shape[0]
    half = p0.shape[0]
    col = BLK // 2
    h = 0 if by_y else 1
    lead = (4,) if by_y else (2, 2)
    outs = [jax.ShapeDtypeStruct(lead + (half, col), F32 if i == 0 else BF) for i in range(4)]
    full = pl.BlockSpec(lead + (half, col), lambda s, t: (0,) * (len(lead) + 2))
    return pl.pallas_call(
        functools.partial(gradient_kernel, by_y),
        grid_spec=pltpu.PrefetchScalarGridSpec(
            num_scalar_prefetch=1,
            grid=(8,),
            in_specs=[
                pl.BlockSpec((2 * n, 2 * half), lambda s, t: (0, 0)),
                pl.BlockSpec((g, 2 * half), lambda s, t: (0, 0)),
                pl.BlockSpec((n, col), lambda s, t: (0, 2 * t[s] + h)),
                pl.BlockSpec((n, col), lambda s, t: (0, 2 * t[s] + h)),
                pl.BlockSpec((half, col), lambda s, t: (0, 2 * t[s] + h)),
                pl.BlockSpec((half, col), lambda s, t: (0, 2 * t[s] + h)),
                pl.BlockSpec((g, col), lambda s, t: (0, 2 * (2 * t[s] + t[8]) + h)),
            ],
            out_specs=[full] * 4,
        ),
        out_shape=outs,
    )(jt, weights, mass, wa, wb, p0, p1, ctf)


def shift(v, axis, size, d):
    return lax.ppermute(v, axis, [((i + d) % size, i) for i in range(size)])


def flip_y(v, bits):
    return lax.ppermute(v, ("yh", "yl"), [(i ^ bits, i) for i in range(4)])


def flip_core(v):
    return lax.ppermute(v, "core", [(0, 1), (1, 0)])


def f32(v):
    return v.astype(F32)


def shards(particles, projections, ctf, group_ids):
    n, f = particles.shape
    rows = projections.shape[0]
    nz = lax.axis_size("z")
    inverse = 4.0 / math.sqrt(f)
    pose_total = rows * nz * 2
    factor = pose_total / (n * 16 * 2 * nz)
    core = lax.axis_index("core")
    x = lax.axis_index("x")
    yh = lax.axis_index("yh")
    z = lax.axis_index("z")
    parity = core[None].astype(jnp.int32)
    ids = group_ids[None, :]

    nb = f // BLK // 2
    mine = lax.dynamic_slice(
        projections.reshape(rows, nb, 2, BLK), (0, 0, core, 0), (rows, nb, 1, BLK)
    ).reshape(rows, nb * BLK)
    hw = nb * BLK // 2

    near = {d: shift(mine, "z", nz, d) for d in (1, -1, 2, -2)}
    far = {d: shift(near[2 * d], "z", nz, d) for d in (1, -1)}
    opp_l = shift(near[2][:, :hw], "z", nz, 2)
    opp_r = shift(near[-2][:, hw:], "z", nz, -2)
    opp = jnp.concatenate([opp_l, opp_r], axis=1)

    first = [mine, near[1], near[2], near[-2], near[-1]]
    second = [far[1], opp, far[-1]]

    def other(blocks):
        stack = jnp.concatenate(blocks, axis=0)
        return flip_y(stack[:, :hw], 1), flip_y(stack[:, hw:], 3)

    f_l, f_r = other(first)
    s_l, s_r = other(second)

    def order(one, two):
        return jnp.concatenate([one[: 3 * rows], two, one[3 * rows :]], axis=0)

    proj_own = order(jnp.concatenate(first, axis=0), jnp.concatenate(second, axis=0))
    proj_oth = jnp.concatenate([order(f_l, s_l), order(f_r, s_r)], axis=1)

    w_send = weighted_call(1 - parity, ids, ctf, particles)
    w_recv = flip_core(w_send)
    w_own = weighted_call(parity, ids, ctf, particles)
    ids_all = jnp.concatenate([ids, flip_core(ids)], axis=1)

    s0, n0 = score_call(parity, w_own, w_recv, proj_own, ctf)
    s1, n1 = score_call(parity, w_own, w_recv, proj_oth, ctf)

    def swap(v):
        got = flip_core(v)
        return jnp.concatenate([got[n:], got[:n]], axis=0)

    r0, r1 = swap(s0), swap(s1)
    m0, m1 = flip_core(n0), flip_core(n1)
    log_norm, weights, mass = softmax_call(inverse, ids_all, (s0, r0, s1, r1, n0, m0, n1, m1))

    steps = jnp.arange(8, dtype=jnp.int32)
    jt = jnp.concatenate([(yh ^ (steps // 4)) * 4 + (x + steps) % 4, parity])
    args = (jt, weights, mass, w_own, w_recv, proj_own, proj_oth, ctf)
    ya = gradient_call(True, *args)
    xb = gradient_call(False, *args)

    ya_sum = ya[0] + f32(flip_y(ya[1], 1)) + f32(flip_y(ya[2], 2)) + f32(flip_y(ya[3], 3))
    xb_sum = xb[0]
    for d in (1, 2, 3):
        xb_sum = xb_sum + f32(shift(xb[d], "x", 4, -d))
    ya_two = ya_sum[0]
    for d in (1, 2, 3):
        ya_two = ya_two + f32(shift(ya_sum[d].astype(BF), "x", 4, -d))
    xb_two = xb_sum[0, 0]
    for a, b in ((0, 1), (1, 0), (1, 1)):
        xb_two = xb_two + f32(flip_y(xb_sum[a, b].astype(BF), 2 * a + b))
    both = jnp.concatenate([ya_two, xb_two], axis=1).astype(BF).reshape(nz, rows, BLK)
    both = lax.dynamic_slice(
        jnp.concatenate([both, both], axis=0), ((nz - z) % nz, 0, 0), (nz, rows, BLK)
    )
    parts = lax.all_to_all(both, "z", 0, 0)
    out = factor * jnp.sum(f32(parts), axis=0)
    return out, log_norm[:, 0]


def solution(mesh):
    fine = jax.sharding.Mesh(mesh.devices.reshape(2, 4, 2, 2, 8), NAMES)
    grp, pose = ("yh", "x", "core"), ("yl", "z")
    return jax.shard_map(
        shards,
        mesh=fine,
        in_specs=(P(grp + pose, None), P(pose, None), P(), P(grp + pose)),
        out_specs=(P(pose, grp), P(grp + pose)),
        check_vma=False,
    )
```

```python
import functools
import math

import jax
import jax.numpy as jnp
from jax import lax
from jax.experimental import pallas as pl
from jax.experimental.pallas import tpu as pltpu
from jax.sharding import PartitionSpec as P

NAMES = ("yh", "x", "core", "yl", "z")
BLK = 1024
COL = BLK // 2
BF = jnp.bfloat16
F32 = jnp.float32
LIMIT = pltpu.CompilerParams(vmem_limit_bytes=24 * 2**20)


def dot_tn(a, b):
    return lax.dot_general(a, b, (((0,), (0,)), ((), ())), preferred_element_type=F32)


def dot_nt(a, b):
    return lax.dot_general(a, b, (((1,), (1,)), ((), ())), preferred_element_type=F32)


def one_hot_t(ids, groups):
    rows = lax.broadcasted_iota(jnp.int32, (groups, ids.shape[1]), 0)
    return jnp.where(rows == ids, 1.0, 0.0).astype(BF)


def split2(v):
    hi = v.astype(BF)
    return hi, (v - hi.astype(F32)).astype(BF)


def split3(v):
    hi = v.astype(BF)
    rest = v - hi.astype(F32)
    mid = rest.astype(BF)
    return hi, mid, (rest - mid.astype(F32)).astype(BF)


def weighted_kernel(par_ref, ids_ref, c0_ref, c1_ref, x0_ref, x1_ref, out_ref):
    hot = one_hot_t(ids_ref[...], c0_ref.shape[0])
    for i, (c_ref, x_ref) in enumerate(((c0_ref, x0_ref), (c1_ref, x1_ref))):
        rows = dot_tn(hot, c_ref[...])
        out = (rows * x_ref[...].astype(F32)).astype(BF)
        for h in range(2):
            out_ref[h, :, i * COL : (i + 1) * COL] = out[:, h * COL : (h + 1) * COL]


def weighted_call(parity, ids, ctf, particles):
    n, f = particles.shape
    g = ctf.shape[0]
    return pl.pallas_call(
        weighted_kernel,
        grid_spec=pltpu.PrefetchScalarGridSpec(
            num_scalar_prefetch=1,
            grid=(f // BLK // 4,),
            in_specs=[
                pl.BlockSpec((1, n), lambda j, p: (0, 0)),
                pl.BlockSpec((g, BLK), lambda j, p: (0, 4 * j + p[0])),
                pl.BlockSpec((g, BLK), lambda j, p: (0, 4 * j + 2 + p[0])),
                pl.BlockSpec((n, BLK), lambda j, p: (0, 4 * j + p[0])),
                pl.BlockSpec((n, BLK), lambda j, p: (0, 4 * j + 2 + p[0])),
            ],
            out_specs=pl.BlockSpec((2, n, BLK), lambda j, p: (0, 0, j)),
        ),
        out_shape=jax.ShapeDtypeStruct((2, n, f // 4), BF),
        compiler_params=LIMIT,
    )(parity, ids, ctf, ctf, particles, particles)


def score_kernel(with_norms, half_ref, wa_ref, wb_ref, p0_ref, p1_ref, *refs):
    s_ref = refs[-2] if with_norms else refs[-1]
    j = pl.program_id(0)
    n = wa_ref.shape[1]
    proj = jnp.where(j == 0, p0_ref[...], p1_ref[...])
    updates = [
        (s_ref, slice(0, n), dot_nt(wa_ref[0], proj)),
        (s_ref, slice(n, 2 * n), dot_nt(wb_ref[0], proj)),
    ]
    if with_norms:
        poses = proj.shape[0]
        g = refs[0].shape[1]
        c = refs[0][0].astype(F32)
        pf = proj.astype(F32)
        quad = dot_nt(
            jnp.concatenate(split2(c * c), axis=0), jnp.concatenate(split2(pf * pf), axis=0)
        )
        dn = (quad[:g, :poses] + quad[g:, :poses]) + (quad[:g, poses:] + quad[g:, poses:])
        updates.append((refs[-1], slice(0, g), dn))

    @pl.when(j == 0)
    def _():
        for ref, rows, v in updates:
            ref[rows, :] = v

    @pl.when(j > 0)
    def _():
        for ref, rows, v in updates:
            ref[rows, :] += v


def score_call(half, own, recv, pieces, ctf=None):
    _, n, f = own.shape
    poses = pieces[0].shape[0]
    wide = f // 2
    ops = [own, recv, *pieces]

    def part(v):
        return pl.BlockSpec((1, v.shape[1], wide), lambda j, h: (h[0], 0, j))

    specs = [part(own), part(recv)]
    if len(pieces) == 1:
        ops = [own, recv, pieces[0], pieces[0]]
        specs += [pl.BlockSpec((poses, wide), lambda j, h, i=i: (0, i)) for i in range(2)]
    else:
        specs += [pl.BlockSpec((poses, wide), lambda j, h: (0, 0))] * 2
    outs = [jax.ShapeDtypeStruct((2 * n, poses), F32)]
    if ctf is not None:
        ops.append(ctf)
        specs.append(part(ctf))
        outs.append(jax.ShapeDtypeStruct((ctf.shape[1], poses), F32))
    return pl.pallas_call(
        functools.partial(score_kernel, ctf is not None),
        grid_spec=pltpu.PrefetchScalarGridSpec(
            num_scalar_prefetch=1,
            grid=(2,),
            in_specs=specs,
            out_specs=[pl.BlockSpec(o.shape, lambda j, h: (0, 0)) for o in outs],
        ),
        out_shape=outs,
        compiler_params=LIMIT,
    )(half, *ops)


def softmax_kernel(inverse, ids_ref, s0, s1, r_ref, norm_ref, log_ref, w_ref, mass_ref):
    n = s0.shape[0] // 2
    g = norm_ref.shape[0]
    mine, got = s0[...] + s1[...], r_ref[...]
    raw = mine + jnp.concatenate([got[n:], got[:n]], axis=0)
    hot = one_hot_t(ids_ref[...], g)
    picked = dot_tn(
        jnp.concatenate([hot, hot, hot], axis=0), jnp.concatenate(split3(norm_ref[...]), axis=0)
    )
    scores = inverse * (raw - 0.5 * picked)
    peak = jnp.max(scores, axis=1, keepdims=True)
    log_norm = peak + jnp.log(jnp.sum(jnp.exp(scores - peak), axis=1, keepdims=True))
    weights = jnp.exp(scores - log_norm).astype(BF)
    log_ref[...] = log_norm[: log_ref.shape[0], :]
    w_ref[...] = weights
    mh, mm, ml = split3(jnp.dot(hot, weights, preferred_element_type=F32))
    mass_ref[...] = jnp.concatenate([mh, mh, mm, mm, ml], axis=0)


def softmax_call(inverse, ids, s0, s1, got, norms):
    rows = ids.shape[1]
    g, poses = norms.shape
    return pl.pallas_call(
        functools.partial(softmax_kernel, inverse),
        out_shape=[
            jax.ShapeDtypeStruct((rows // 2, 1), F32),
            jax.ShapeDtypeStruct((rows, poses), BF),
            jax.ShapeDtypeStruct((5 * g, poses), BF),
        ],
        compiler_params=LIMIT,
    )(ids, s0, s1, got, norms)


def gradient_kernel(w_ref, mass_ref, wa_ref, wb_ref, p_ref, ctf_ref, out_ref):
    n = wa_ref.shape[1]
    rows = out_ref.shape[3]
    for x in range(4):
        cols = slice(x * COL, (x + 1) * COL)
        acc = dot_tn(w_ref[:n, :], wa_ref[0, :, cols]) + dot_tn(w_ref[n:, :], wb_ref[0, :, cols])
        c = ctf_ref[0, :, cols].astype(F32)
        ch, cl = split2(c * c)
        corr = dot_tn(mass_ref[...], jnp.concatenate([ch, cl, ch, cl, ch], axis=0))
        v = (acc - p_ref[:, cols].astype(F32) * corr).astype(BF)
        for yl in range(2):
            out_ref[0, yl, x] = v[yl * rows : (yl + 1) * rows]


def gradient_call(h, weights, mass, wa, wb, proj, ctf):
    _, n, f = wa.shape
    poses = proj.shape[0]
    wide = f // 2

    def part(v):
        return pl.BlockSpec((1, v.shape[1], wide), lambda a: (h, 0, a))

    def whole(v):
        return pl.BlockSpec(v.shape, lambda a: (0, 0))

    return pl.pallas_call(
        gradient_kernel,
        grid=(2,),
        in_specs=[
            whole(weights),
            whole(mass),
            part(wa),
            part(wb),
            pl.BlockSpec((poses, wide), lambda a: (0, a)),
            part(ctf),
        ],
        out_specs=pl.BlockSpec((1, 2, 4, poses // 2, COL), lambda a: (a, 0, 0, 0, 0)),
        out_shape=jax.ShapeDtypeStruct((2, 2, 4, poses // 2, COL), BF),
        compiler_params=LIMIT,
    )(weights, mass, wa, wb, proj, ctf)


def flip_x(v, bits):
    return lax.ppermute(v, "x", [(i ^ bits, i) for i in range(4)])


def flip_core(v):
    return lax.ppermute(v, "core", [(0, 1), (1, 0)])


def f32(v):
    return v.astype(F32)


def shards(particles, projections, ctf, group_ids):
    n, f = particles.shape
    rows = projections.shape[0]
    nz = lax.axis_size("z")
    poses = rows * nz * 2
    inverse = 4.0 / math.sqrt(f)
    factor = poses / (n * 16 * 2 * nz)
    core = lax.axis_index("core")
    odd = lax.axis_index("x") % 2
    parity = core[None].astype(jnp.int32)
    half = odd[None].astype(jnp.int32)
    ids = group_ids[None, :]

    nb = f // BLK // 2
    quarter = lax.dynamic_slice(
        projections.reshape(rows, nb, 4, COL), (0, 0, 2 * core + odd, 0), (rows, nb, 1, COL)
    ).reshape(rows, nb * COL)
    copies = jnp.broadcast_to(quarter, (2 * nz, rows, nb * COL))
    own = lax.all_to_all(copies, ("yl", "z"), 0, 0).reshape(poses, nb * COL)
    w_own = weighted_call(parity, ids, ctf, particles)
    ids_oth = flip_core(ids)
    w_recv = weighted_call(parity, ids_oth, ctf, flip_core(particles))
    ids_all = jnp.concatenate([ids, ids_oth], axis=1)
    ctf_own = lax.dynamic_index_in_dim(
        ctf.reshape(ctf.shape[0], nb, 2, 2, COL), core, axis=2, keepdims=False
    )
    ctf_own = ctf_own.transpose(2, 0, 1, 3).reshape(2, ctf.shape[0], nb * COL)

    own, w_own, w_recv, ids_all, ctf_own = lax.optimization_barrier(
        (own, w_own, w_recv, ids_all, ctf_own)
    )

    mid = nb * COL // 2
    oth = [flip_x(own[:, :mid], 1), flip_x(own[:, mid:], 3)]

    w_own = pltpu.with_memory_space_constraint(w_own, pltpu.HBM)
    w_recv = pltpu.with_memory_space_constraint(w_recv, pltpu.HBM)
    s0, norms = score_call(half, w_own, w_recv, [own], ctf_own)
    norms = norms + flip_core(norms)
    norms = norms + flip_x(norms, 1)
    (s1,) = score_call(1 - half, w_own, w_recv, oth)
    got = flip_core(s0 + s1)
    log_norm, weights, mass = softmax_call(inverse, ids_all, s0, s1, got, norms)

    last = []
    for h in range(2):
        proj = jnp.where(odd == h, own, jnp.concatenate(oth, axis=1))
        part = gradient_call(h, weights, mass, w_own, w_recv, proj, ctf_own)
        part = part.reshape(16, poses // 2, COL)
        part = lax.all_to_all(part, ("yh", "yl", "x"), 0, 0)
        last.append(jnp.sum(f32(part), axis=0).astype(BF))
    last = jnp.concatenate(last, axis=1).reshape(nz, rows, BLK)
    parts = lax.all_to_all(last, "z", 0, 0)
    out = factor * jnp.sum(f32(parts), axis=0)
    return out, log_norm[:, 0]


def solution(mesh):
    fine = jax.sharding.Mesh(mesh.devices.reshape(2, 4, 2, 2, 8), NAMES)
    grp, pose = ("yh", "x", "core"), ("yl", "z")
    return jax.shard_map(
        shards,
        mesh=fine,
        in_specs=(P(grp + pose, None), P(pose, None), P(), P(grp + pose)),
        out_specs=(P(pose, grp), P(grp + pose)),
        check_vma=False,
    )
```

```python
import functools
import math

import jax
import jax.numpy as jnp
from jax import lax
from jax.experimental import pallas as pl
from jax.experimental.pallas import tpu as pltpu
from jax.sharding import PartitionSpec as P

NAMES = ("yh", "x", "core", "yl", "z")
BLK = 1024
COL = BLK // 2
BF = jnp.bfloat16
F32 = jnp.float32
LIMIT = pltpu.CompilerParams(vmem_limit_bytes=24 * 2**20)


def dot_tn(a, b):
    return lax.dot_general(a, b, (((0,), (0,)), ((), ())), preferred_element_type=F32)


def dot_nt(a, b):
    return lax.dot_general(a, b, (((1,), (1,)), ((), ())), preferred_element_type=F32)


def one_hot_t(ids, groups):
    rows = lax.broadcasted_iota(jnp.int32, (groups, ids.shape[1]), 0)
    return jnp.where(rows == ids, 1.0, 0.0).astype(BF)


def split2(v):
    hi = v.astype(BF)
    return hi, (v - hi.astype(F32)).astype(BF)


def split3(v):
    hi = v.astype(BF)
    rest = v - hi.astype(F32)
    mid = rest.astype(BF)
    return hi, mid, (rest - mid.astype(F32)).astype(BF)


def weighted_kernel(par_ref, ids_ref, c0_ref, c1_ref, x0_ref, x1_ref, out_ref):
    hot = one_hot_t(ids_ref[...], c0_ref.shape[0])
    for i, (c_ref, x_ref) in enumerate(((c0_ref, x0_ref), (c1_ref, x1_ref))):
        rows = dot_tn(hot, c_ref[...])
        out = (rows * x_ref[...].astype(F32)).astype(BF)
        for h in range(2):
            out_ref[h, :, i * COL : (i + 1) * COL] = out[:, h * COL : (h + 1) * COL]


def weighted_call(parity, ids, ctf, particles):
    n, f = particles.shape
    g = ctf.shape[0]
    return pl.pallas_call(
        weighted_kernel,
        grid_spec=pltpu.PrefetchScalarGridSpec(
            num_scalar_prefetch=1,
            grid=(f // BLK // 4,),
            in_specs=[
                pl.BlockSpec((1, n), lambda j, p: (0, 0)),
                pl.BlockSpec((g, BLK), lambda j, p: (0, 4 * j + p[0])),
                pl.BlockSpec((g, BLK), lambda j, p: (0, 4 * j + 2 + p[0])),
                pl.BlockSpec((n, BLK), lambda j, p: (0, 4 * j + p[0])),
                pl.BlockSpec((n, BLK), lambda j, p: (0, 4 * j + 2 + p[0])),
            ],
            out_specs=pl.BlockSpec((2, n, BLK), lambda j, p: (0, 0, j)),
        ),
        out_shape=pltpu.HBM((2, n, f // 4), BF),
        compiler_params=LIMIT,
    )(parity, ids, ctf, ctf, particles, particles)


def score_kernel(at_ref, wa_ref, wb_ref, p0_ref, p1_ref, c0, c1, c2, c3, s_ref):
    j = pl.program_id(0)
    n = wa_ref.shape[1]
    g, poses = c0.shape[0], p0_ref.shape[0]
    proj = jnp.where(j == 0, p0_ref[...], p1_ref[...])
    c = jnp.concatenate([r[...] for r in (c0, c1, c2, c3)], axis=1).astype(F32)
    pf = proj.astype(F32)
    quad = dot_nt(jnp.concatenate(split2(c * c), axis=0), jnp.concatenate(split2(pf * pf), axis=0))
    updates = (
        (slice(0, n), dot_nt(wa_ref[0], proj)),
        (slice(n, 2 * n), dot_nt(wb_ref[0], proj)),
        (
            slice(2 * n, 2 * n + g),
            (quad[:g, :poses] + quad[g:, :poses]) + (quad[:g, poses:] + quad[g:, poses:]),
        ),
    )

    @pl.when(j == 0)
    def _():
        for rows, v in updates:
            s_ref[rows, :] = v

    @pl.when(j > 0)
    def _():
        for rows, v in updates:
            s_ref[rows, :] += v


def score_call(half, parity, own, recv, pieces, ctf):
    _, n, f = own.shape
    poses = pieces[0].shape[0]
    g = ctf.shape[0]
    wide = f // 2
    part = pl.BlockSpec((1, n, wide), lambda j, t: (t[0], 0, j))
    if len(pieces) == 1:
        pieces = pieces * 2
        specs = [pl.BlockSpec((poses, wide), lambda j, t, i=i: (0, i)) for i in range(2)]
    else:
        specs = [pl.BlockSpec((poses, wide), lambda j, t: (0, 0))] * 2
    specs += [
        pl.BlockSpec((g, COL), lambda j, t, i=i: (0, 4 * (4 * j + i) + 2 * t[1] + t[0])) for i in range(4)
    ]
    return pl.pallas_call(
        score_kernel,
        grid_spec=pltpu.PrefetchScalarGridSpec(
            num_scalar_prefetch=1,
            grid=(2,),
            in_specs=[part, part, *specs],
            out_specs=pl.BlockSpec((2 * n + g, poses), lambda j, t: (0, 0)),
        ),
        out_shape=jax.ShapeDtypeStruct((2 * n + g, poses), F32),
        compiler_params=LIMIT,
    )(jnp.concatenate([half, parity]), own, recv, *pieces, ctf, ctf, ctf, ctf)


def softmax_kernel(inverse, ids_ref, s_ref, r_ref, log_ref, w_ref, mass_ref):
    n = log_ref.shape[0]
    g = s_ref.shape[0] - 2 * n
    mine, got = s_ref[...], r_ref[...]
    raw = mine[: 2 * n] + jnp.concatenate([got[n : 2 * n], got[:n]], axis=0)
    norms = mine[2 * n :] + got[2 * n :]
    hot = one_hot_t(ids_ref[...], g)
    picked = dot_tn(
        jnp.concatenate([hot, hot, hot], axis=0), jnp.concatenate(split3(norms), axis=0)
    )
    scores = inverse * (raw - 0.5 * picked)
    peak = jnp.max(scores, axis=1, keepdims=True)
    log_norm = peak + jnp.log(jnp.sum(jnp.exp(scores - peak), axis=1, keepdims=True))
    weights = jnp.exp(scores - log_norm).astype(BF)
    log_ref[...] = log_norm[: log_ref.shape[0], :]
    w_ref[...] = weights
    mh, mm, ml = split3(jnp.dot(hot, weights, preferred_element_type=F32))
    mass_ref[...] = jnp.concatenate([mh, mh, mm, mm, ml], axis=0)


def softmax_call(inverse, ids, mine, got):
    rows = ids.shape[1]
    g, poses = mine.shape[0] - rows, mine.shape[1]
    return pl.pallas_call(
        functools.partial(softmax_kernel, inverse),
        out_shape=[
            jax.ShapeDtypeStruct((rows // 2, 1), F32),
            jax.ShapeDtypeStruct((rows, poses), BF),
            jax.ShapeDtypeStruct((5 * g, poses), BF),
        ],
        compiler_params=LIMIT,
    )(ids, mine, got)


def gradient_kernel(at_ref, w_ref, mass_ref, wa_ref, wb_ref, p0_ref, p1_ref, c0, c1, c2, c3, out_ref):
    n = wa_ref.shape[1]
    rows = out_ref.shape[3]
    own = pl.program_id(0) == at_ref[0]
    for x, c_ref in enumerate((c0, c1, c2, c3)):
        cols = slice(x * COL, (x + 1) * COL)
        acc = dot_tn(w_ref[:n, :], wa_ref[0, :, cols]) + dot_tn(w_ref[n:, :], wb_ref[0, :, cols])
        c = c_ref[...].astype(F32)
        ch, cl = split2(c * c)
        corr = dot_tn(mass_ref[...], jnp.concatenate([ch, cl, ch, cl, ch], axis=0))
        proj = jnp.where(own, p0_ref[:, cols], p1_ref[:, cols])
        v = (acc - proj.astype(F32) * corr).astype(BF)
        for i in range(2):
            out_ref[0, at_ref[2] ^ i, x] = v[i * rows : (i + 1) * rows]


def gradient_call(at, weights, mass, wa, wb, own, oth, ctf):
    _, n, f = wa.shape
    poses = own.shape[0]
    wide = f // 2
    g = ctf.shape[0]

    def whole(v):
        return pl.BlockSpec(v.shape, lambda h, a, t: (0, 0))

    part = pl.BlockSpec((1, n, wide), lambda h, a, t: (h, 0, a))
    proj = pl.BlockSpec((poses, wide), lambda h, a, t: (0, a))
    ctfs = [
        pl.BlockSpec((g, COL), lambda h, a, t, i=i: (0, 4 * (4 * a + i) + 2 * t[1] + h)) for i in range(4)
    ]
    return pl.pallas_call(
        gradient_kernel,
        grid_spec=pltpu.PrefetchScalarGridSpec(
            num_scalar_prefetch=1,
            grid=(2, 2),
            in_specs=[whole(weights), whole(mass), part, part, proj, proj, *ctfs],
            out_specs=pl.BlockSpec((1, 2, 4, poses // 2, COL), lambda h, a, t: (a, 0, 0, 0, h)),
        ),
        out_shape=pltpu.VMEM((2, 2, 4, poses // 2, BLK), BF),
        compiler_params=LIMIT,
    )(at, weights, mass, wa, wb, own, oth, ctf, ctf, ctf, ctf)


def copies_kernel(nb, at_ref, p_ref, out_ref):
    for j in range(nb):
        cols = pl.ds(pl.multiple_of((4 * j + at_ref[0]) * COL, COL), COL)
        v = p_ref[:, cols]
        for i in range(out_ref.shape[0]):
            out_ref[i, :, j * COL : (j + 1) * COL] = v


def copies_call(at, projections, nb, count):
    rows = projections.shape[0]
    return pl.pallas_call(
        functools.partial(copies_kernel, nb),
        in_specs=[
            pl.BlockSpec(memory_space=pltpu.SMEM),
            pl.BlockSpec(memory_space=pltpu.VMEM),
        ],
        out_specs=pl.BlockSpec(memory_space=pltpu.VMEM),
        out_shape=pltpu.VMEM((count, rows, nb * COL), BF),
        compiler_params=LIMIT,
    )(at, projections)


def flip_x(v, bits):
    return lax.ppermute(v, "x", [(i ^ bits, i) for i in range(4)])


def flip_y(v, bits):
    return lax.ppermute(v, ("yh", "yl"), [(i ^ bits, i) for i in range(4)])


def flip_core(v):
    return lax.ppermute(v, "core", [(0, 1), (1, 0)])


def f32(v):
    return v.astype(F32)


def shards(particles, projections, ctf, group_ids):
    n, f = particles.shape
    rows = projections.shape[0]
    nz = lax.axis_size("z")
    poses = rows * nz * 2
    inverse = 4.0 / math.sqrt(f)
    factor = poses / (n * 16 * 2 * nz)
    core = lax.axis_index("core")
    odd = lax.axis_index("x") % 2
    parity = core[None].astype(jnp.int32)
    half = odd[None].astype(jnp.int32)
    ids = group_ids[None, :]

    nb = f // BLK // 2
    copies = copies_call((2 * core + odd)[None].astype(jnp.int32), projections, nb, nz)
    own = lax.all_to_all(copies, "z", 0, 0).reshape(poses // 2, nb * COL)

    w_own = weighted_call(parity, ids, ctf, in_hbm(particles))
    ids_oth = flip_core(ids)
    w_recv = weighted_call(parity, ids_oth, ctf, in_hbm(flip_core(particles)))
    ids_all = jnp.concatenate([ids, ids_oth], axis=1)
    own, w_own, w_recv, ids_all = lax.optimization_barrier((own, w_own, w_recv, ids_all))
    w_own, w_recv = in_hbm(w_own), in_hbm(w_recv)

    mid = nb * COL // 2
    cols = [own[:, :mid], own[:, mid:]]
    by_y = [flip_y(v, b) for v, b in zip(cols, (1, 3))]
    by_x = [flip_x(v, b) for v, b in zip(cols, (1, 3))]
    both = [
        [flip_x(by_y[i][:, : mid // 2], b), flip_y(by_x[i][:, mid // 2 :], b)] for i, b in enumerate((1, 3))
    ]
    at = jnp.concatenate([half, parity, lax.axis_index("yl")[None].astype(jnp.int32)])
    own = jnp.concatenate([own, jnp.concatenate(by_y, axis=1)], axis=0)
    oth = [jnp.concatenate([by_x[i], jnp.concatenate(both[i], axis=1)], axis=0) for i in range(2)]

    s0 = score_call(half, parity, w_own, w_recv, [own], ctf)
    s1 = score_call(1 - half, parity, w_own, w_recv, oth, ctf)
    mine = s0 + s1
    log_norm, weights, mass = softmax_call(inverse, ids_all, mine, flip_core(mine))
    part = gradient_call(at, weights, mass, w_own, w_recv, own, jnp.concatenate(oth, axis=1), ctf)
    part = part.reshape(16, poses // 2, BLK)
    part, log_norm = lax.optimization_barrier((part, log_norm[:, 0]))
    part = lax.all_to_all(part, ("yh", "yl", "x"), 0, 0)
    last = jnp.sum(f32(part), axis=0).astype(BF).reshape(nz, rows, BLK)
    parts = lax.all_to_all(last, "z", 0, 0)
    out = factor * jnp.sum(f32(parts), axis=0)
    return out, log_norm


def in_hbm(v):
    return pltpu.with_memory_space_constraint(v, pltpu.HBM)


def solution(mesh):
    fine = jax.sharding.Mesh(mesh.devices.reshape(2, 4, 2, 2, 8), NAMES)
    grp, pose = ("yh", "x", "core"), ("yl", "z")
    return jax.shard_map(
        shards,
        mesh=fine,
        in_specs=(P(grp + pose, None), P(pose, None), P(), P(grp + pose)),
        out_specs=(P(pose, grp), P(grp + pose)),
        check_vma=False,
    )
```

```python
import functools
import math

import jax
import jax.numpy as jnp
from jax import lax
from jax.experimental import pallas as pl
from jax.experimental.pallas import tpu as pltpu
from jax.sharding import PartitionSpec as P

NAMES = ("yh", "x", "core", "yl", "z")
BLK = 1024
COL = BLK // 2
BF = jnp.bfloat16
F32 = jnp.float32
LIMIT = pltpu.CompilerParams(vmem_limit_bytes=24 * 2**20)


def dot_tn(a, b):
    return lax.dot_general(a, b, (((0,), (0,)), ((), ())), preferred_element_type=F32)


def dot_nt(a, b):
    return lax.dot_general(a, b, (((1,), (1,)), ((), ())), preferred_element_type=F32)


def one_hot_t(ids, groups):
    rows = lax.broadcasted_iota(jnp.int32, (groups, ids.shape[1]), 0)
    return jnp.where(rows == ids, 1.0, 0.0).astype(BF)


def split2(v):
    hi = v.astype(BF)
    return hi, (v - hi.astype(F32)).astype(BF)


def split3(v):
    hi = v.astype(BF)
    rest = v - hi.astype(F32)
    mid = rest.astype(BF)
    return hi, mid, (rest - mid.astype(F32)).astype(BF)


def weighted_kernel(par_ref, ids_ref, c0_ref, c1_ref, x0_ref, x1_ref, out_ref):
    hot = one_hot_t(ids_ref[...], c0_ref.shape[0])
    for i, (c_ref, x_ref) in enumerate(((c0_ref, x0_ref), (c1_ref, x1_ref))):
        rows = dot_tn(hot, c_ref[...])
        out = (rows * x_ref[...].astype(F32)).astype(BF)
        for h in range(2):
            out_ref[h, :, i * COL : (i + 1) * COL] = out[:, h * COL : (h + 1) * COL]


def weighted_call(parity, ids, ctf, particles):
    n, f = particles.shape
    g = ctf.shape[0]
    return pl.pallas_call(
        weighted_kernel,
        grid_spec=pltpu.PrefetchScalarGridSpec(
            num_scalar_prefetch=1,
            grid=(f // BLK // 4,),
            in_specs=[
                pl.BlockSpec((1, n), lambda j, p: (0, 0)),
                pl.BlockSpec((g, BLK), lambda j, p: (0, 4 * j + p[0])),
                pl.BlockSpec((g, BLK), lambda j, p: (0, 4 * j + 2 + p[0])),
                pl.BlockSpec((n, BLK), lambda j, p: (0, 4 * j + p[0])),
                pl.BlockSpec((n, BLK), lambda j, p: (0, 4 * j + 2 + p[0])),
            ],
            out_specs=pl.BlockSpec((2, n, BLK), lambda j, p: (0, 0, j)),
        ),
        out_shape=pltpu.HBM((2, n, f // 4), BF),
        compiler_params=LIMIT,
    )(parity, ids, ctf, ctf, particles, particles)


def score_kernel(at_ref, wa_ref, wb_ref, p0_ref, p1_ref, c0, c1, c2, c3, s_ref):
    j = pl.program_id(0)
    n = wa_ref.shape[1]
    g, poses = c0.shape[0], p0_ref.shape[0]
    proj = jnp.where(j == 0, p0_ref[...], p1_ref[...])
    c = jnp.concatenate([r[...] for r in (c0, c1, c2, c3)], axis=1).astype(F32)
    pf = proj.astype(F32)
    quad = dot_nt(jnp.concatenate(split2(c * c), axis=0), jnp.concatenate(split2(pf * pf), axis=0))
    updates = (
        (slice(0, n), dot_nt(wa_ref[0], proj)),
        (slice(n, 2 * n), dot_nt(wb_ref[0], proj)),
        (
            slice(2 * n, 2 * n + g),
            (quad[:g, :poses] + quad[g:, :poses]) + (quad[:g, poses:] + quad[g:, poses:]),
        ),
    )

    @pl.when(j == 0)
    def _():
        for rows, v in updates:
            s_ref[rows, :] = v

    @pl.when(j > 0)
    def _():
        for rows, v in updates:
            s_ref[rows, :] += v


def score_call(half, parity, own, recv, pieces, ctf):
    _, n, f = own.shape
    poses = pieces[0].shape[0]
    g = ctf.shape[0]
    wide = f // 2
    part = pl.BlockSpec((1, n, wide), lambda j, t: (t[0], 0, j))
    if len(pieces) == 1:
        pieces = pieces * 2
        specs = [pl.BlockSpec((poses, wide), lambda j, t, i=i: (0, i)) for i in range(2)]
    else:
        specs = [pl.BlockSpec((poses, wide), lambda j, t: (0, 0))] * 2
    specs += [
        pl.BlockSpec((g, COL), lambda j, t, i=i: (0, 4 * (4 * j + i) + 2 * t[1] + t[0])) for i in range(4)
    ]
    return pl.pallas_call(
        score_kernel,
        grid_spec=pltpu.PrefetchScalarGridSpec(
            num_scalar_prefetch=1,
            grid=(2,),
            in_specs=[part, part, *specs],
            out_specs=pl.BlockSpec((2 * n + g, poses), lambda j, t: (0, 0)),
        ),
        out_shape=jax.ShapeDtypeStruct((2 * n + g, poses), F32),
        compiler_params=LIMIT,
    )(jnp.concatenate([half, parity]), own, recv, *pieces, ctf, ctf, ctf, ctf)


def softmax_kernel(inverse, ids_ref, s_ref, r_ref, log_ref, w_ref, mass_ref):
    n = log_ref.shape[0]
    g = s_ref.shape[0] - 2 * n
    mine, got = s_ref[...], r_ref[...]
    raw = mine[: 2 * n] + jnp.concatenate([got[n : 2 * n], got[:n]], axis=0)
    norms = mine[2 * n :] + got[2 * n :]
    hot = one_hot_t(ids_ref[...], g)
    picked = dot_tn(
        jnp.concatenate([hot, hot, hot], axis=0), jnp.concatenate(split3(norms), axis=0)
    )
    scores = inverse * (raw - 0.5 * picked)
    peak = jnp.max(scores, axis=1, keepdims=True)
    log_norm = peak + jnp.log(jnp.sum(jnp.exp(scores - peak), axis=1, keepdims=True))
    weights = jnp.exp(scores - log_norm).astype(BF)
    log_ref[...] = log_norm[: log_ref.shape[0], :]
    w_ref[...] = weights
    mh, mm, ml = split3(jnp.dot(hot, weights, preferred_element_type=F32))
    mass_ref[...] = jnp.concatenate([mh, mh, mm, mm, ml], axis=0)


def softmax_call(inverse, ids, mine, got):
    rows = ids.shape[1]
    g, poses = mine.shape[0] - rows, mine.shape[1]
    return pl.pallas_call(
        functools.partial(softmax_kernel, inverse),
        out_shape=[
            jax.ShapeDtypeStruct((rows // 2, 1), F32),
            jax.ShapeDtypeStruct((rows, poses), BF),
            jax.ShapeDtypeStruct((5 * g, poses), BF),
        ],
        compiler_params=LIMIT,
    )(ids, mine, got)


def gradient_kernel(at_ref, w_ref, mass_ref, wa_ref, wb_ref, p0_ref, p1_ref, c0, c1, c2, c3, out_ref):
    n = wa_ref.shape[1]
    rows = out_ref.shape[3]
    own = pl.program_id(0) == at_ref[0]
    for x, c_ref in enumerate((c0, c1, c2, c3)):
        cols = slice(x * COL, (x + 1) * COL)
        acc = dot_tn(w_ref[:n, :], wa_ref[0, :, cols]) + dot_tn(w_ref[n:, :], wb_ref[0, :, cols])
        c = c_ref[...].astype(F32)
        ch, cl = split2(c * c)
        corr = dot_tn(mass_ref[...], jnp.concatenate([ch, cl, ch, cl, ch], axis=0))
        proj = jnp.where(own, p0_ref[:, cols], p1_ref[:, cols])
        v = (acc - proj.astype(F32) * corr).astype(BF)
        for i in range(2):
            out_ref[0, at_ref[2] ^ i, x] = v[i * rows : (i + 1) * rows]


def gradient_call(at, weights, mass, wa, wb, own, oth, ctf):
    _, n, f = wa.shape
    poses = own.shape[0]
    wide = f // 2
    g = ctf.shape[0]

    def whole(v):
        return pl.BlockSpec(v.shape, lambda h, a, t: (0, 0))

    part = pl.BlockSpec((1, n, wide), lambda h, a, t: (h, 0, a))
    proj = pl.BlockSpec((poses, wide), lambda h, a, t: (0, a))
    ctfs = [
        pl.BlockSpec((g, COL), lambda h, a, t, i=i: (0, 4 * (4 * a + i) + 2 * t[1] + h)) for i in range(4)
    ]
    return pl.pallas_call(
        gradient_kernel,
        grid_spec=pltpu.PrefetchScalarGridSpec(
            num_scalar_prefetch=1,
            grid=(2, 2),
            in_specs=[whole(weights), whole(mass), part, part, proj, proj, *ctfs],
            out_specs=pl.BlockSpec((1, 2, 4, poses // 2, COL), lambda h, a, t: (a, 0, 0, 0, h)),
        ),
        out_shape=pltpu.VMEM((2, 2, 4, poses // 2, BLK), BF),
        compiler_params=LIMIT,
    )(at, weights, mass, wa, wb, own, oth, ctf, ctf, ctf, ctf)


def copies_kernel(nb, at_ref, p_ref, out_ref):
    for j in range(nb):
        cols = pl.ds(pl.multiple_of((4 * j + at_ref[0]) * COL, COL), COL)
        v = p_ref[:, cols]
        for i in range(out_ref.shape[0]):
            out_ref[i, :, j * COL : (j + 1) * COL] = v


def copies_call(at, projections, nb, count):
    rows = projections.shape[0]
    return pl.pallas_call(
        functools.partial(copies_kernel, nb),
        in_specs=[
            pl.BlockSpec(memory_space=pltpu.SMEM),
            pl.BlockSpec(memory_space=pltpu.VMEM),
        ],
        out_specs=pl.BlockSpec(memory_space=pltpu.VMEM),
        out_shape=pltpu.VMEM((count, rows, nb * COL), BF),
        compiler_params=LIMIT,
    )(at, projections)


def flip_x(v, bits):
    return lax.ppermute(v, "x", [(i ^ bits, i) for i in range(4)])


def flip_y(v, bits):
    return lax.ppermute(v, ("yh", "yl"), [(i ^ bits, i) for i in range(4)])


def flip_core(v):
    return lax.ppermute(v, "core", [(0, 1), (1, 0)])


def f32(v):
    return v.astype(F32)


def shards(particles, projections, ctf, group_ids):
    n, f = particles.shape
    rows = projections.shape[0]
    nz = lax.axis_size("z")
    poses = rows * nz * 2
    inverse = 4.0 / math.sqrt(f)
    factor = poses / (n * 16 * 2 * nz)
    core = lax.axis_index("core")
    odd = lax.axis_index("x") % 2
    parity = core[None].astype(jnp.int32)
    half = odd[None].astype(jnp.int32)
    ids = group_ids[None, :]

    nb = f // BLK // 2
    copies = copies_call((2 * core + odd)[None].astype(jnp.int32), projections, nb, nz)
    up = [list(range(nz)), list(range(2 * nz - 1, nz - 1, -1))]
    own = lax.all_to_all(copies, ("core", "z"), 0, 0, axis_index_groups=up)

    w_own = weighted_call(parity, ids, ctf, in_hbm(particles))
    ids_oth = flip_core(ids)
    w_recv = weighted_call(parity, ids_oth, ctf, in_hbm(flip_core(particles)))
    ids_all = jnp.concatenate([ids, ids_oth], axis=1)
    own, w_own, w_recv, ids_all = lax.optimization_barrier((own, w_own, w_recv, ids_all))
    w_own, w_recv = in_hbm(w_own), in_hbm(w_recv)
    own = jnp.where(core == 1, own[::-1], own).reshape(poses // 2, nb * COL)

    mid = nb * COL // 2
    cols = [own[:, :mid], own[:, mid:]]
    by_y = [flip_y(v, b) for v, b in zip(cols, (1, 3))]
    by_x = [flip_x(v, b) for v, b in zip(cols, (1, 3))]
    both = [
        [flip_x(by_y[i][:, : mid // 2], b), flip_y(by_x[i][:, mid // 2 :], b)] for i, b in enumerate((1, 3))
    ]
    at = jnp.concatenate([half, parity, lax.axis_index("yl")[None].astype(jnp.int32)])
    own = jnp.concatenate([own, jnp.concatenate(by_y, axis=1)], axis=0)
    oth = [jnp.concatenate([by_x[i], jnp.concatenate(both[i], axis=1)], axis=0) for i in range(2)]

    s0 = score_call(half, parity, w_own, w_recv, [own], ctf)
    s1 = score_call(1 - half, parity, w_own, w_recv, oth, ctf)
    mine = s0 + s1
    log_norm, weights, mass = softmax_call(inverse, ids_all, mine, flip_core(mine))
    part = gradient_call(at, weights, mass, w_own, w_recv, own, jnp.concatenate(oth, axis=1), ctf)
    part = part.reshape(16, poses // 2, BLK)
    part, log_norm = lax.optimization_barrier((part, log_norm[:, 0]))
    part = lax.all_to_all(part, ("yh", "yl", "x"), 0, 0)
    last = jnp.sum(f32(part), axis=0).astype(BF).reshape(nz, rows, BLK)
    parts = lax.all_to_all(last[::-1], "z", 0, 0, axis_index_groups=[list(range(nz))[::-1]])
    out = factor * jnp.sum(f32(parts), axis=0)
    return out, log_norm


def in_hbm(v):
    return pltpu.with_memory_space_constraint(v, pltpu.HBM)


def solution(mesh):
    fine = jax.sharding.Mesh(mesh.devices.reshape(2, 4, 2, 2, 8), NAMES)
    grp, pose = ("yh", "x", "core"), ("yl", "z")
    return jax.shard_map(
        shards,
        mesh=fine,
        in_specs=(P(grp + pose, None), P(pose, None), P(), P(grp + pose)),
        out_specs=(P(pose, grp), P(grp + pose)),
        check_vma=False,
    )
```

```python
import functools
import math

import jax
import jax.numpy as jnp
from jax import lax
from jax.experimental import pallas as pl
from jax.experimental.pallas import tpu as pltpu
from jax.sharding import PartitionSpec as P

NAMES = ("yh", "x", "core", "yl", "z")
BLK = 1024
COL = BLK // 2
BF = jnp.bfloat16
F32 = jnp.float32
LIMIT = pltpu.CompilerParams(vmem_limit_bytes=24 * 2**20)


def dot_tn(a, b):
    return lax.dot_general(a, b, (((0,), (0,)), ((), ())), preferred_element_type=F32)


def dot_nt(a, b):
    return lax.dot_general(a, b, (((1,), (1,)), ((), ())), preferred_element_type=F32)


def one_hot_t(ids, groups):
    rows = lax.broadcasted_iota(jnp.int32, (groups, ids.shape[1]), 0)
    return jnp.where(rows == ids, 1.0, 0.0).astype(BF)


def split2(v):
    hi = v.astype(BF)
    return hi, (v - hi.astype(F32)).astype(BF)


def split3(v):
    hi = v.astype(BF)
    rest = v - hi.astype(F32)
    mid = rest.astype(BF)
    return hi, mid, (rest - mid.astype(F32)).astype(BF)


def weighted_kernel(par_ref, ids_ref, c0_ref, c1_ref, x0_ref, x1_ref, out_ref):
    hot = one_hot_t(ids_ref[...], c0_ref.shape[0])
    for i, (c_ref, x_ref) in enumerate(((c0_ref, x0_ref), (c1_ref, x1_ref))):
        rows = dot_tn(hot, c_ref[...])
        out = (rows * x_ref[...].astype(F32)).astype(BF)
        for h in range(2):
            out_ref[h, :, i * COL : (i + 1) * COL] = out[:, h * COL : (h + 1) * COL]


def weighted_call(parity, ids, ctf, particles):
    n, f = particles.shape
    g = ctf.shape[0]
    return pl.pallas_call(
        weighted_kernel,
        grid_spec=pltpu.PrefetchScalarGridSpec(
            num_scalar_prefetch=1,
            grid=(f // BLK // 4,),
            in_specs=[
                pl.BlockSpec((1, n), lambda j, p: (0, 0)),
                pl.BlockSpec((g, BLK), lambda j, p: (0, 4 * j + p[0])),
                pl.BlockSpec((g, BLK), lambda j, p: (0, 4 * j + 2 + p[0])),
                pl.BlockSpec((n, BLK), lambda j, p: (0, 4 * j + p[0])),
                pl.BlockSpec((n, BLK), lambda j, p: (0, 4 * j + 2 + p[0])),
            ],
            out_specs=pl.BlockSpec((2, n, BLK), lambda j, p: (0, 0, j)),
        ),
        out_shape=pltpu.HBM((2, n, f // 4), BF),
        compiler_params=LIMIT,
    )(parity, ids, ctf, ctf, particles, particles)


def score_kernel(at_ref, wa_ref, wb_ref, p0_ref, p1_ref, c0, c1, c2, c3, s_ref):
    j = pl.program_id(0)
    n = wa_ref.shape[1]
    g, poses = c0.shape[0], p0_ref.shape[0]
    proj = jnp.where(j == 0, p0_ref[...], p1_ref[...])
    c = jnp.concatenate([r[...] for r in (c0, c1, c2, c3)], axis=1).astype(F32)
    pf = proj.astype(F32)
    quad = dot_nt(jnp.concatenate(split2(c * c), axis=0), jnp.concatenate(split2(pf * pf), axis=0))
    updates = (
        (slice(0, n), dot_nt(wa_ref[0], proj)),
        (slice(n, 2 * n), dot_nt(wb_ref[0], proj)),
        (
            slice(2 * n, 2 * n + g),
            (quad[:g, :poses] + quad[g:, :poses]) + (quad[:g, poses:] + quad[g:, poses:]),
        ),
    )

    @pl.when(j == 0)
    def _():
        for rows, v in updates:
            s_ref[rows, :] = v

    @pl.when(j > 0)
    def _():
        for rows, v in updates:
            s_ref[rows, :] += v


def score_call(half, parity, own, recv, pieces, ctf):
    _, n, f = own.shape
    poses = pieces[0].shape[0]
    g = ctf.shape[0]
    wide = f // 2
    part = pl.BlockSpec((1, n, wide), lambda j, t: (t[0], 0, j))
    if len(pieces) == 1:
        pieces = pieces * 2
        specs = [pl.BlockSpec((poses, wide), lambda j, t, i=i: (0, i)) for i in range(2)]
    else:
        specs = [pl.BlockSpec((poses, wide), lambda j, t: (0, 0))] * 2
    specs += [
        pl.BlockSpec((g, COL), lambda j, t, i=i: (0, 4 * (4 * j + i) + 2 * t[1] + t[0])) for i in range(4)
    ]
    return pl.pallas_call(
        score_kernel,
        grid_spec=pltpu.PrefetchScalarGridSpec(
            num_scalar_prefetch=1,
            grid=(2,),
            in_specs=[part, part, *specs],
            out_specs=pl.BlockSpec((2 * n + g, poses), lambda j, t: (0, 0)),
        ),
        out_shape=jax.ShapeDtypeStruct((2 * n + g, poses), F32),
        compiler_params=LIMIT,
    )(jnp.concatenate([half, parity]), own, recv, *pieces, ctf, ctf, ctf, ctf)


def softmax_kernel(inverse, ids_ref, s_ref, r_ref, log_ref, w_ref, mass_ref):
    n = log_ref.shape[0]
    g = s_ref.shape[0] - 2 * n
    mine, got = s_ref[...], r_ref[...]
    raw = mine[: 2 * n] + jnp.concatenate([got[n : 2 * n], got[:n]], axis=0)
    norms = mine[2 * n :] + got[2 * n :]
    hot = one_hot_t(ids_ref[...], g)
    picked = dot_tn(
        jnp.concatenate([hot, hot, hot], axis=0), jnp.concatenate(split3(norms), axis=0)
    )
    scores = inverse * (raw - 0.5 * picked)
    peak = jnp.max(scores, axis=1, keepdims=True)
    log_norm = peak + jnp.log(jnp.sum(jnp.exp(scores - peak), axis=1, keepdims=True))
    weights = jnp.exp(scores - log_norm).astype(BF)
    log_ref[...] = log_norm[: log_ref.shape[0], :]
    w_ref[...] = weights
    mh, mm, ml = split3(jnp.dot(hot, weights, preferred_element_type=F32))
    mass_ref[...] = jnp.concatenate([mh, mh, mm, mm, ml], axis=0)


def softmax_call(inverse, ids, mine, got):
    rows = ids.shape[1]
    g, poses = mine.shape[0] - rows, mine.shape[1]
    return pl.pallas_call(
        functools.partial(softmax_kernel, inverse),
        out_shape=[
            jax.ShapeDtypeStruct((rows // 2, 1), F32),
            jax.ShapeDtypeStruct((rows, poses), BF),
            jax.ShapeDtypeStruct((5 * g, poses), BF),
        ],
        compiler_params=LIMIT,
    )(ids, mine, got)


def gradient_kernel(at_ref, w_ref, mass_ref, wa_ref, wb_ref, p0_ref, p1_ref, c0, c1, c2, c3, out_ref):
    n = wa_ref.shape[1]
    rows = out_ref.shape[3]
    own = pl.program_id(0) == at_ref[0]
    for x, c_ref in enumerate((c0, c1, c2, c3)):
        cols = slice(x * COL, (x + 1) * COL)
        acc = dot_tn(w_ref[:n, :], wa_ref[0, :, cols]) + dot_tn(w_ref[n:, :], wb_ref[0, :, cols])
        c = c_ref[...].astype(F32)
        ch, cl = split2(c * c)
        corr = dot_tn(mass_ref[...], jnp.concatenate([ch, cl, ch, cl, ch], axis=0))
        proj = jnp.where(own, p0_ref[:, cols], p1_ref[:, cols])
        v = (acc - proj.astype(F32) * corr).astype(BF)
        for i in range(2):
            out_ref[0, at_ref[2] ^ i, x] = v[i * rows : (i + 1) * rows]


def gradient_call(at, weights, mass, wa, wb, own, oth, ctf):
    _, n, f = wa.shape
    poses = own.shape[0]
    wide = f // 2
    g = ctf.shape[0]

    def whole(v):
        return pl.BlockSpec(v.shape, lambda h, a, t: (0, 0))

    part = pl.BlockSpec((1, n, wide), lambda h, a, t: (h, 0, a))
    proj = pl.BlockSpec((poses, wide), lambda h, a, t: (0, a))
    ctfs = [
        pl.BlockSpec((g, COL), lambda h, a, t, i=i: (0, 4 * (4 * a + i) + 2 * t[1] + h)) for i in range(4)
    ]
    return pl.pallas_call(
        gradient_kernel,
        grid_spec=pltpu.PrefetchScalarGridSpec(
            num_scalar_prefetch=1,
            grid=(2, 2),
            in_specs=[whole(weights), whole(mass), part, part, proj, proj, *ctfs],
            out_specs=pl.BlockSpec((1, 2, 4, poses // 2, COL), lambda h, a, t: (a, 0, 0, 0, h)),
        ),
        out_shape=pltpu.VMEM((2, 2, 4, poses // 2, BLK), BF),
        compiler_params=LIMIT,
    )(at, weights, mass, wa, wb, own, oth, ctf, ctf, ctf, ctf)


def copies_kernel(nb, at_ref, p_ref, out_ref):
    for j in range(nb):
        cols = pl.ds(pl.multiple_of((4 * j + at_ref[0]) * COL, COL), COL)
        v = p_ref[:, cols]
        for i in range(out_ref.shape[0]):
            out_ref[i, :, j * COL : (j + 1) * COL] = v


def copies_call(at, projections, nb, count):
    rows = projections.shape[0]
    return pl.pallas_call(
        functools.partial(copies_kernel, nb),
        in_specs=[
            pl.BlockSpec(memory_space=pltpu.SMEM),
            pl.BlockSpec(memory_space=pltpu.VMEM),
        ],
        out_specs=pl.BlockSpec(memory_space=pltpu.VMEM),
        out_shape=pltpu.VMEM((count, rows, nb * COL), BF),
        compiler_params=LIMIT,
    )(at, projections)


def flip_x(v, bits):
    return lax.ppermute(v, "x", [(i ^ bits, i) for i in range(4)])


def flip_y(v, bits):
    return lax.ppermute(v, ("yh", "yl"), [(i ^ bits, i) for i in range(4)])


def flip_core(v):
    return lax.ppermute(v, "core", [(0, 1), (1, 0)])


def f32(v):
    return v.astype(F32)


def shards(particles, projections, ctf, group_ids):
    n, f = particles.shape
    rows = projections.shape[0]
    nz = lax.axis_size("z")
    poses = rows * nz * 2
    inverse = 4.0 / math.sqrt(f)
    factor = poses / (n * 16 * 2 * nz)
    core = lax.axis_index("core")
    odd = lax.axis_index("x") % 2
    parity = core[None].astype(jnp.int32)
    half = odd[None].astype(jnp.int32)
    ids = group_ids[None, :]

    nb = f // BLK // 2
    copies = copies_call((2 * core + odd)[None].astype(jnp.int32), projections, nb, nz)
    up = [list(range(nz)), list(range(2 * nz - 1, nz - 1, -1))]
    own = lax.all_to_all(copies, ("core", "z"), 0, 0, axis_index_groups=up)

    w_own = weighted_call(parity, ids, ctf, in_hbm(particles))
    ids_oth = flip_core(ids)
    w_recv = weighted_call(parity, ids_oth, ctf, in_hbm(flip_core(particles)))
    ids_all = jnp.concatenate([ids, ids_oth], axis=1)
    own, w_own, w_recv, ids_all = lax.optimization_barrier((own, w_own, w_recv, ids_all))
    w_own, w_recv = in_hbm(w_own), in_hbm(w_recv)
    own = jnp.where(core == 1, own[::-1], own).reshape(poses // 2, nb * COL)

    mid = nb * COL // 2
    cols = [own[:, :mid], own[:, mid:]]
    by_y = [flip_y(v, b) for v, b in zip(cols, (1, 3))]
    by_x = [flip_x(v, b) for v, b in zip(cols, (1, 3))]
    both = [
        [flip_x(by_y[i][:, : mid // 2], b), flip_y(by_x[i][:, mid // 2 :], b)] for i, b in enumerate((1, 3))
    ]
    at = jnp.concatenate([half, parity, lax.axis_index("yl")[None].astype(jnp.int32)])
    own = jnp.concatenate([own, jnp.concatenate(by_y, axis=1)], axis=0)
    oth = [jnp.concatenate([by_x[i], jnp.concatenate(both[i], axis=1)], axis=0) for i in range(2)]

    s0 = score_call(half, parity, w_own, w_recv, [own], ctf)
    s1 = score_call(1 - half, parity, w_own, w_recv, oth, ctf)
    mine = s0 + s1
    log_norm, weights, mass = softmax_call(inverse, ids_all, mine, flip_core(mine))
    part = gradient_call(at, weights, mass, w_own, w_recv, own, jnp.concatenate(oth, axis=1), ctf)
    part = part.reshape(16, poses // 2, BLK)
    part = lax.all_to_all(part, ("yh", "yl", "x"), 0, 0)
    last = jnp.sum(f32(part), axis=0).astype(BF).reshape(nz, rows, BLK)
    parts = lax.all_to_all(last[::-1], "z", 0, 0, axis_index_groups=[list(range(nz))[::-1]])
    parts, log_norm = lax.optimization_barrier((parts, log_norm))
    out = factor * jnp.sum(f32(parts), axis=0)
    return out, log_norm[:, 0]


def in_hbm(v):
    return pltpu.with_memory_space_constraint(v, pltpu.HBM)


def solution(mesh):
    fine = jax.sharding.Mesh(mesh.devices.reshape(2, 4, 2, 2, 8), NAMES)
    grp, pose = ("yh", "x", "core"), ("yl", "z")
    return jax.shard_map(
        shards,
        mesh=fine,
        in_specs=(P(grp + pose, None), P(pose, None), P(), P(grp + pose)),
        out_specs=(P(pose, grp), P(grp + pose)),
        check_vma=False,
    )
```
